32 devices in a mesh: req: 8 (over z, x), mlp: 4 (over y, core).
Axes of the slice: x: 2, y: 2, z: 4, core: 2. Of those that a mesh axis runs over, the one named last changes fastest.
Arguments:
- tokens: bfloat16 [8192, 2048], P('req', 'mlp'), may hold values from -40 to 40, as said below
- norm_gain_vector: bfloat16 [2048], replicated, may hold values from 0.099609375 to 1.8984375
- gate_weight: bfloat16 [2048, 3584], P(None, 'mlp'), may hold values from -0.125 to 0.125
- up_weight: bfloat16 [2048, 3584], P(None, 'mlp'), may hold values from -0.125 to 0.125
- down_weight: bfloat16 [3584, 2048], P('mlp'), may hold values from -0.09375 to 0.09375
- gate_up_input_maps: bfloat16 [8, 2048, 32], P('req'), may hold values from -0.125 to 0.125
- gate_up_output_maps: bfloat16 [8, 2, 16, 3584], P('req', None, None, 'mlp'), may hold values from -1.5 to 1.5
- down_input_maps: bfloat16 [8, 3584, 16], P('req', 'mlp'), may hold values from -0.09375 to 0.09375
- down_output_maps: bfloat16 [8, 16, 2048], P('req'), may hold values from -1.5 to 1.5
- lengths: int32 [8, 4], replicated, may hold values from 0 to 1024, as said below
- request_adapter_slot: int32 [8, 4], replicated, may hold values from 0 to 7
- selected: int32 [8], replicated, may hold values from 0 to 7, as said below
Outputs:
- layer_out: bfloat16 [8192, 2048], P('req', 'mlp')
The draws below stay inside these ranges and needn't reach their ends.
Inputs may be any that keep to these rules, and one draw needn't show every extreme that they name: Each row of lengths sums to a multiple of 64 from 64 to 1024; some row sums to exactly 1024 and holds all of it in one slot; all rows together sum to 4096. Slots may hold zero tokens. `selected`: 8 different adapter ids; adapter a is owned by index a // 1 of req. `tokens`: entries of order one, some rows and features larger than others.
All inputs are finite; a program needn't handle non-finite values.
Results may differ from the reference program's by a relative error of at most 0.006.
Values may be sent and summed in bfloat16 or wider, within the bound.
A program may use at most 128 MiB of HBM per device.

```python
import math
import jax
import jax.numpy as jnp
from jax import lax

MODEL_WIDTH = 2048
HIDDEN_UNITS = 3584
ADAPTER_RANK = 16
TOK_DEV = 512
REQ_DEV = 4
BLK = 64
CAP = 1024
ROWS = 8192
TOKENS = 4096
ADAPTER_TOTAL = 8
SEL = 8
N_REQ = 8
N_MLP = 4


def draw_tokens(key, part):
    key_noise, key_rows, key_cols = jax.random.split(jax.random.fold_in(key, 3), 3)
    noise_base = jax.random.truncated_normal(key_noise, -4.0, 4.0, (ROWS, MODEL_WIDTH), jnp.float32)
    spread_log = math.log(3.0)
    row_scale = jnp.exp(jax.random.uniform(key_rows, (ROWS, 1), jnp.float32, -spread_log, spread_log))
    col_scale = jnp.exp(jax.random.uniform(key_cols, (1, MODEL_WIDTH), jnp.float32, -spread_log, spread_log))
    return (noise_base * row_scale * col_scale).astype(jnp.bfloat16)


def draw_lengths(key, part):
    groups = TOKENS // TOK_DEV
    balanced = groups
    half_count = groups // 2
    key_order, key_pairs, key_cuts = jax.random.split(jax.random.fold_in(key, 7), 3)
    order = jax.random.permutation(key_order, groups)
    deltas = jax.random.randint(key_pairs, (half_count,), -(balanced - 1), balanced, dtype=jnp.int32)
    firsts = balanced + deltas
    seconds = balanced - deltas
    firsts = firsts.at[0].set(2 * balanced).at[1].set(balanced)
    seconds = seconds.at[0].set(1).at[1].set(balanced - 1)
    paired = jnp.stack([firsts, seconds], axis=1).reshape(groups)
    counts = jnp.zeros((groups,), jnp.int32).at[order].set(paired)
    totals = counts * BLK
    cuts = jax.random.randint(key_cuts, (groups, REQ_DEV - 1), 0, totals[:, None] + 1, dtype=jnp.int32)
    full_group = (totals == CAP)[:, None]
    cuts = jnp.where(full_group, totals[:, None], cuts)
    cuts = jnp.sort(cuts, axis=1)
    bounds = jnp.concatenate([jnp.zeros((groups, 1), jnp.int32), cuts, totals[:, None]], axis=1)
    return (bounds[:, 1:] - bounds[:, :-1]).astype(jnp.int32)


def draw_selected(key, part):
    key_middle, key_order = jax.random.split(jax.random.fold_in(key, 5), 2)
    middle = jax.random.permutation(key_middle, ADAPTER_TOTAL - 2).astype(jnp.int32) + 1
    ends = jnp.array([0, ADAPTER_TOTAL - 1], jnp.int32)
    picked = jnp.concatenate([ends, middle[:SEL - 2]], axis=0)
    shuffle = jax.random.permutation(key_order, SEL)
    return jnp.take(picked, shuffle, axis=0).astype(jnp.int32)


def with_ends(values, key, least, largest):
    longest = values.shape.index(max(values.shape))
    spots = []
    for shift in (0, 1):
        where = [jax.random.randint(jax.random.fold_in(key, axis), (), 0, length) for axis, length in enumerate(values.shape)]
        where[longest] = (where[longest] + shift) % values.shape[longest]
        spots.append(tuple(where))
    return values.at[spots[0]].set(least).at[spots[1]].set(largest)


def block_levels(stream_key, shape, cuts, low, high):
    factor_of = 1.0
    for dim, blocks in cuts:
        draws = jax.random.uniform(jax.random.fold_in(jax.random.fold_in(stream_key, 6), dim), (blocks,), jnp.float32, low / len(cuts), high / len(cuts))
        factor_of = factor_of * jnp.repeat(jnp.exp(draws), shape[dim] // blocks).reshape((-1,) + (1,) * (len(shape) - 1 - dim))
    return factor_of


def normal_values(rng, dims, width, most, pieces=(), held_as=jnp.bfloat16):
    values = width * jax.random.normal(rng, dims, jnp.float32)
    if pieces:
        values = values * block_levels(rng, dims, pieces, -0.22, 0.18)
    return jnp.clip(values, -most, most).astype(held_as)


def setup_inputs(seed: int = 0) -> dict:
    key_list = jax.random.split(jax.random.key(seed), 13)
    return {
        "tokens": draw_tokens(jax.random.fold_in(key_list[12], 71), 0),
        "norm_gain_vector": jnp.clip(1.0 + 0.18 * jax.random.normal(key_list[1], (MODEL_WIDTH,), jnp.float32), 0.099609375, 1.8984375).astype(jnp.bfloat16),
        "gate_weight": normal_values(key_list[2], (MODEL_WIDTH, HIDDEN_UNITS), MODEL_WIDTH ** -0.5, 0.125, ((1, 4),)),
        "up_weight": normal_values(key_list[3], (MODEL_WIDTH, HIDDEN_UNITS), MODEL_WIDTH ** -0.5, 0.125, ((1, 4),)),
        "down_weight": normal_values(key_list[4], (HIDDEN_UNITS, MODEL_WIDTH), HIDDEN_UNITS ** -0.5, 0.09375, ((0, 4),)),
        "gate_up_input_maps": normal_values(key_list[5], (ADAPTER_TOTAL, MODEL_WIDTH, 2 * ADAPTER_RANK), MODEL_WIDTH ** -0.5, 0.125, ((0, 8),)),
        "gate_up_output_maps": normal_values(key_list[6], (ADAPTER_TOTAL, 2, ADAPTER_RANK, HIDDEN_UNITS), ADAPTER_RANK ** -0.5, 1.5, ((0, 8), (3, 4))),
        "down_input_maps": normal_values(key_list[7], (ADAPTER_TOTAL, HIDDEN_UNITS, ADAPTER_RANK), HIDDEN_UNITS ** -0.5, 0.09375, ((0, 8), (1, 4))),
        "down_output_maps": normal_values(key_list[8], (ADAPTER_TOTAL, ADAPTER_RANK, MODEL_WIDTH), ADAPTER_RANK ** -0.5, 1.5, ((0, 8),)),
        "lengths": draw_lengths(jax.random.fold_in(key_list[12], 71), 0),
        "request_adapter_slot": with_ends(jax.random.randint(key_list[10], (N_REQ, REQ_DEV), 0, SEL), jax.random.fold_in(key_list[10], 1), 0, SEL - 1).astype(jnp.int32),
        "selected": draw_selected(jax.random.fold_in(key_list[12], 71), 0),
    }


EPSILON = 1e-06

def slot_table(owners, positions, lengths, request_adapter_slot, token_count):
    lens = jnp.take(lengths, owners, axis=0)
    req_ends = jnp.cumsum(lens, axis=1)
    starts = req_ends - lens
    inside = (positions[:, None] >= starts) & (positions[:, None] < req_ends)
    adapter_ids = jnp.take(request_adapter_slot, owners, axis=0)
    picked = lax.optimization_barrier(jnp.sum(jnp.where(inside, adapter_ids, 0), axis=1))
    live = jnp.any(inside, axis=1)
    onehot = (picked[:, None] == jnp.arange(token_count, dtype=jnp.int32)[None, :]) & live[:, None]
    return onehot.astype(jnp.float32)

def reference(tokens, norm_gain_vector, gate_weight, up_weight, down_weight, gate_up_input_maps, gate_up_output_maps, down_input_maps, down_output_maps, lengths, request_adapter_slot, selected):
    highest = lax.Precision.HIGHEST
    selected_input_maps = jnp.take(gate_up_input_maps, selected, axis=0).astype(jnp.float32)
    selected_output_maps = jnp.take(gate_up_output_maps, selected, axis=0).astype(jnp.float32)
    sel_da = jnp.take(down_input_maps, selected, axis=0).astype(jnp.float32)
    sel_db = jnp.take(down_output_maps, selected, axis=0).astype(jnp.float32)
    totals = lax.optimization_barrier(jnp.sum(lengths, axis=1))
    gain = norm_gain_vector.astype(jnp.float32)
    piece = HIDDEN_UNITS // N_MLP

    def per_device(item):
        device, block = item
        positions = jnp.arange(CAP, dtype=jnp.int32)
        owners = jnp.zeros((CAP,), jnp.int32) + device.astype(jnp.int32)
        onehot = slot_table(owners, positions, lengths, request_adapter_slot, SEL)
        values = block.astype(jnp.float32)
        mean_square = lax.optimization_barrier(jnp.mean(values * values, axis=1, keepdims=True))
        normed_input = (values * lax.rsqrt(mean_square + EPSILON) * gain).astype(jnp.bfloat16)
        low_rank_term = jnp.einsum('ec,mch->emh', normed_input.astype(jnp.float32), selected_input_maps, precision=highest) * onehot[:, :, None]
        low_rank_term = lax.optimization_barrier(low_rank_term.astype(jnp.bfloat16)).astype(jnp.float32)
        gate_sum = jnp.dot(normed_input, gate_weight, preferred_element_type=jnp.float32) + jnp.einsum('vca,can->vn', low_rank_term[:, :, :ADAPTER_RANK], selected_output_maps[:, 0], precision=highest)
        up_sum = jnp.dot(normed_input, up_weight, preferred_element_type=jnp.float32) + jnp.einsum('vca,can->vn', low_rank_term[:, :, ADAPTER_RANK:], selected_output_maps[:, 1], precision=highest)
        hidden = (jax.nn.silu(gate_sum) * up_sum).astype(jnp.bfloat16)
        hidden_wide = hidden.astype(jnp.float32)
        branch = jnp.zeros((CAP, MODEL_WIDTH), jnp.float32)
        for shard in range(N_MLP):
            low = shard * piece
            hidden_part = hidden[:, low:low + piece]
            down_rank = jnp.einsum('tf,sfr->tsr', hidden_wide[:, low:low + piece], sel_da[:, low:low + piece], precision=highest) * onehot[:, :, None]
            part = jnp.dot(hidden_part, down_weight[low:low + piece], preferred_element_type=jnp.float32) + jnp.einsum('tsr,srd->td', down_rank, sel_db, precision=highest)
            part = lax.optimization_barrier(part.astype(jnp.bfloat16)).astype(jnp.float32)
            branch = branch + part
        branch = lax.optimization_barrier(branch.astype(jnp.bfloat16)).astype(jnp.float32)
        row_valid = positions < totals[device]
        return jnp.where(row_valid[:, None], values + branch, values).astype(jnp.bfloat16)
    result = lax.map(per_device, (jnp.arange(N_REQ, dtype=jnp.int32), tokens.reshape(N_REQ, CAP, MODEL_WIDTH)))
    return result.reshape(ROWS, MODEL_WIDTH)
```

```python
import functools

import jax
import jax.numpy as jnp
from jax import lax
from jax.experimental import pallas as pl
from jax.experimental.pallas import tpu as pltpu
from jax.sharding import PartitionSpec as P

EPSILON = 1e-06
CHUNKS = 4
MESH = pl.DeviceIdType.MESH
NT = (((1,), (1,)), ((), ()))


def kernel(
    groups,
    owned,
    rank,
    slots,
    ids_ref,
    total_ref,
    tokens_ref,
    gain_ref,
    gate_ref,
    up_ref,
    down_ref,
    pack_ref,
    low_ref,
    high_ref,
    out_ref,
    gate_v,
    up_v,
    down_v,
    whole,
    normed,
    hidden,
    maps,
    maps_sib,
    a_sel,
    bg_sel,
    bu_sel,
    da_sel,
    db_sel,
    own_part,
    sib_out,
    sib_in,
    far_out,
    far_in,
    ad_s,
    ad_r,
    af_s,
    af_r,
    ts_s,
    ts_r,
    tc_s,
    tc_r,
    tf_s,
    tf_r,
    rs_s,
    rs_r,
    rc_s,
    rc_r,
    local_sem,
):
    r = lax.axis_index("req")
    m = lax.axis_index("mlp")
    half = lax.rem(m, 2)
    sib = m + 1 - 2 * half
    side = m // 2
    far = m + 2 - 4 * side
    diag = sib + 2 - 4 * side
    rows, cols = tokens_ref.shape
    rc = rows // CHUNKS
    hwidth = maps_sib.shape[2]
    inner = gate_v.shape[1]
    prow = pack_ref.shape[0]

    def local(i, src, dst):
        return pltpu.make_async_copy(src, dst, local_sem.at[i])

    def remote(src, dst, ss, rs, axis, dev):
        return pltpu.make_async_remote_copy(
            src_ref=src,
            dst_ref=dst,
            send_sem=ss,
            recv_sem=rs,
            device_id={axis: dev},
            device_id_type=MESH,
        )

    def rows_of(k):
        return pl.ds(pl.multiple_of(k * rc, rc), rc)

    def slot_of(g):
        return maps.at[g]

    def ad_copy(i):
        return remote(
            pack_ref, slot_of(r), ad_s.at[i], ad_r.at[i], "req", lax.rem(r + i, groups)
        )

    def ad_wait(i):
        src = lax.rem(r + groups - i, groups)
        return remote(pack_ref, slot_of(src), ad_s.at[i], ad_r.at[i], "req", src)

    def af_copy(i):
        src = lax.rem(r + groups - i, groups)
        return remote(
            maps.at[src, :, pl.ds(0, hwidth)],
            maps_sib.at[src],
            af_s.at[i],
            af_r.at[i],
            "mlp",
            sib,
        )

    def tok_sib(k, who):
        return remote(
            tokens_ref.at[rows_of(k)], whole.at[who, rows_of(k)], ts_s.at[k], ts_r.at[k], "mlp", sib
        )

    def tok_far(k, who):
        return remote(
            tokens_ref.at[rows_of(k)], whole.at[who, rows_of(k)], tc_s.at[k], tc_r.at[k], "mlp", far
        )

    def tok_fwd(k, who):
        return remote(
            whole.at[far, rows_of(k)], whole.at[who, rows_of(k)], tf_s.at[k], tf_r.at[k], "mlp", sib
        )

    def part_sib(k):
        return remote(sib_out.at[k], sib_in.at[k], rs_s.at[k], rs_r.at[k], "mlp", sib)

    def part_far(k):
        return remote(far_out.at[k], far_in.at[k], rc_s.at[k], rc_r.at[k], "mlp", far)

    w_copies = [
        local(0, gate_ref, gate_v),
        local(1, up_ref, up_v),
        local(2, down_ref, down_v),
        local(3, tokens_ref, whole.at[m]),
        local(4, pack_ref, slot_of(r)),
    ]

    barrier = pltpu.get_barrier_semaphore()

    def greet(i, carry):
        pl.semaphore_signal(
            barrier, inc=1, device_id={"req": lax.rem(r + i, groups)}, device_id_type=MESH
        )
        return carry

    lax.fori_loop(1, groups, greet, 0)
    pl.semaphore_signal(barrier, inc=1, device_id={"mlp": sib}, device_id_type=MESH)
    pl.semaphore_signal(barrier, inc=1, device_id={"mlp": far}, device_id_type=MESH)
    pl.semaphore_wait(barrier, groups + 1)

    def each(n, start=0):
        def deco(f):
            def body(i, carry):
                f(i)
                return carry

            lax.fori_loop(start, n, body, 0)

        return deco

    @each(CHUNKS)
    def _(k):
        tok_far(k, m).start()
        tok_sib(k, m).start()

    @each(groups, 1)
    def _(i):
        ad_copy(i).start()

    for j in (4, 3, 0, 1, 2):
        w_copies[j].start()
    w_copies[4].wait()
    w_copies[3].wait()
    af_copy(0).start()

    def pass_on(k):
        tok_far(k, far).wait_recv()
        tok_fwd(k, far).start()

    pass_on(0)

    @each(groups, 1)
    def _(i):
        ad_wait(i).wait_recv()
        af_copy(i).start()

    @each(groups)
    def _(i):
        af_copy(i).wait_recv()

    span = slots * rank
    bg_sel[...] = jnp.zeros_like(bg_sel)
    bu_sel[...] = jnp.zeros_like(bu_sel)
    mine = pl.ds(pl.multiple_of(half * hwidth, hwidth), hwidth)
    other = pl.ds(pl.multiple_of((1 - half) * hwidth, hwidth), hwidth)
    per = prow // owned
    for q in range(slots):
        g = ids_ref[0, q]
        at = pl.ds(q * rank, rank)
        at2 = pl.ds(span + q * rank, rank)
        row0 = ids_ref[1, q] * per if owned > 1 else 0
        for dst, part in ((mine, maps), (other, maps_sib)):
            a_sel[at, dst] = part[g, pl.ds(row0, rank), 0:hwidth]
            a_sel[at2, dst] = part[g, pl.ds(row0 + rank, rank), 0:hwidth]
            db = part[g, pl.ds(row0 + 2 * rank, rank), 0:hwidth]
            db_sel[at, dst] = db
            db_sel[at2, dst] = db
        bg_sel[at, :] = maps[g, pl.ds(row0, rank), hwidth : hwidth + inner]
        bu_sel[at2, :] = maps[g, pl.ds(row0 + rank, rank), hwidth : hwidth + inner]
        da = maps[g, pl.ds(row0 + 2 * rank, rank), hwidth : hwidth + inner]
        da_sel[at, :] = da
        da_sel[at2, :] = da
    for j in (0, 1, 2):
        w_copies[j].wait()

    parts = whole.shape[0]
    f32 = jnp.float32

    def reduce_far(k):
        part_sib(k).wait_recv()
        far_out[k] = (own_part[k, 0] + sib_in[k, 0].astype(f32)).astype(jnp.bfloat16)
        part_far(k).start()

    @each(CHUNKS)
    def _(k):
        here = rows_of(k)

        @pl.when(k < CHUNKS - 1)
        def _():
            pass_on(k + 1)

        tok_sib(k, sib).wait_recv()
        tok_fwd(k, diag).wait_recv()
        squares = jnp.zeros((rc, 1), f32)
        for b in range(parts):
            x = whole[b, here, :].astype(f32)
            squares += jnp.sum(x * x, axis=1, keepdims=True)
        scale = lax.rsqrt(squares / (parts * cols) + EPSILON)
        for b in range(parts):
            x = whole[b, here, :].astype(f32)
            gain = gain_ref[:, b * cols : (b + 1) * cols].astype(f32)
            normed[:, b * cols : (b + 1) * cols] = (x * scale * gain).astype(jnp.bfloat16)
        at = lax.broadcasted_iota(jnp.int32, (rc, 2 * span), 0) + k * rc
        live = (at >= low_ref[...]) & (at < high_ref[...])
        low_rank = lax.dot_general(normed[...], a_sel[...], NT, preferred_element_type=f32)
        low_rank = jnp.where(live, low_rank, 0.0).astype(jnp.bfloat16)
        for n0 in range(0, inner, 256):
            n1 = min(n0 + 256, inner)
            g = jnp.dot(normed[...], gate_v[:, n0:n1], preferred_element_type=f32)
            g += jnp.dot(low_rank, bg_sel[:, n0:n1], preferred_element_type=f32)
            u = jnp.dot(normed[...], up_v[:, n0:n1], preferred_element_type=f32)
            u += jnp.dot(low_rank, bu_sel[:, n0:n1], preferred_element_type=f32)
            hidden[:, n0:n1] = (jax.nn.silu(g) * u).astype(jnp.bfloat16)
        down_rank = lax.dot_general(hidden[...], da_sel[...], NT, preferred_element_type=f32)
        down_rank = jnp.where(live, down_rank, 0.0)
        coarse = down_rank.astype(jnp.bfloat16).astype(f32)
        lane = lax.broadcasted_iota(jnp.int32, (rc, 2 * span), 1)
        down_rank = jnp.where(lane < span, coarse, down_rank - coarse).astype(jnp.bfloat16)

        def part_of(b):
            there = pl.ds(pl.multiple_of(b * cols, cols), cols)
            return jnp.dot(hidden[...], down_v[:, there], preferred_element_type=f32) + jnp.dot(
                down_rank, db_sel[:, there], preferred_element_type=f32
            )

        sib_out[k, 0] = part_of(diag).astype(jnp.bfloat16)
        sib_out[k, 1] = part_of(sib).astype(jnp.bfloat16)
        part_sib(k).start()
        own_part[k, 0] = part_of(far)

        @pl.when(k > 0)
        def _():
            reduce_far(k - 1)

        own_part[k, 1] = part_of(m)

    reduce_far(CHUNKS - 1)
    total = total_ref[0]

    @each(CHUNKS)
    def _(k):
        here = rows_of(k)
        part_far(k).wait_recv()
        branch = own_part[k, 1] + sib_in[k, 1].astype(f32) + far_in[k].astype(f32)
        branch = branch.astype(jnp.bfloat16).astype(f32)
        at = lax.broadcasted_iota(jnp.int32, (rc, cols), 0) + k * rc
        x = whole[m, here, :].astype(f32)
        out_ref[here, :] = jnp.where(at < total, x + branch, x).astype(out_ref.dtype)

    @each(CHUNKS)
    def _(k):
        tok_far(k, m).wait_send()
        tok_sib(k, m).wait_send()
        tok_fwd(k, far).wait_send()
        part_sib(k).wait_send()
        part_far(k).wait_send()

    @each(groups, 1)
    def _(i):
        ad_copy(i).wait_send()

    @each(groups)
    def _(i):
        af_copy(i).wait_send()


def on_device(
    tokens,
    norm_gain_vector,
    gate_weight,
    up_weight,
    down_weight,
    gate_up_input_maps,
    gate_up_output_maps,
    down_input_maps,
    down_output_maps,
    lengths,
    request_adapter_slot,
    selected,
):
    groups = lax.axis_size("req")
    r = lax.axis_index("req")
    m = lax.axis_index("mlp")
    parts = lax.axis_size("mlp")
    rows, cols = tokens.shape
    owned, rank, width = down_output_maps.shape
    inner = gate_weight.shape[1]
    slots = lengths.shape[1]
    span = slots * rank
    hwidth = width // 2
    bf16 = jnp.bfloat16

    shared = jnp.concatenate(
        [jnp.swapaxes(gate_up_input_maps, 1, 2), down_output_maps], axis=1
    )
    shared = lax.dynamic_slice_in_dim(shared, (m % 2) * hwidth, hwidth, axis=2)
    own = jnp.concatenate(
        [
            gate_up_output_maps.reshape(owned, 2 * rank, inner),
            jnp.swapaxes(down_input_maps, 1, 2),
        ],
        axis=1,
    )
    pack = jnp.concatenate([shared, own], axis=2).reshape(owned * 3 * rank, hwidth + inner)

    lens = lengths[r]
    ends = jnp.cumsum(lens)
    starts = ends - lens
    ids = selected[request_adapter_slot[r]]
    ids = jnp.stack([ids // owned, ids % owned]).astype(jnp.int32)
    low = jnp.tile(jnp.repeat(starts, rank), 2).reshape(1, 2 * span)
    high = jnp.tile(jnp.repeat(ends, rank), 2).reshape(1, 2 * span)
    total = ends[slots - 1 :]

    rc = rows // CHUNKS
    vm, sm, hbm = (
        pl.BlockSpec(memory_space=s) for s in (pltpu.VMEM, pltpu.SMEM, pl.ANY)
    )
    dma = pltpu.SemaphoreType.DMA
    return pl.pallas_call(
        functools.partial(kernel, groups, owned, rank, slots),
        out_shape=jax.ShapeDtypeStruct((rows, cols), tokens.dtype),
        in_specs=[sm, sm, hbm, vm, hbm, hbm, hbm, hbm, vm, vm],
        out_specs=vm,
        scratch_shapes=[
            pltpu.VMEM((width, inner), bf16),
            pltpu.VMEM((width, inner), bf16),
            pltpu.VMEM((inner, width), bf16),
            pltpu.VMEM((parts, rows, cols), bf16),
            pltpu.VMEM((rc, width), bf16),
            pltpu.VMEM((rc, inner), bf16),
            pltpu.VMEM((groups,) + pack.shape, bf16),
            pltpu.VMEM((groups, pack.shape[0], hwidth), bf16),
            pltpu.VMEM((2 * span, width), bf16),
            pltpu.VMEM((2 * span, inner), bf16),
            pltpu.VMEM((2 * span, inner), bf16),
            pltpu.VMEM((2 * span, inner), bf16),
            pltpu.VMEM((2 * span, width), bf16),
            pltpu.VMEM((CHUNKS, 2, rc, cols), jnp.float32),
            pltpu.VMEM((CHUNKS, 2, rc, cols), bf16),
            pltpu.VMEM((CHUNKS, 2, rc, cols), bf16),
            pltpu.VMEM((CHUNKS, rc, cols), bf16),
            pltpu.VMEM((CHUNKS, rc, cols), bf16),
            dma((groups,)),
            dma((groups,)),
            dma((groups,)),
            dma((groups,)),
        ]
        + [dma((CHUNKS,)) for _ in range(10)]
        + [dma((5,))],
        compiler_params=pltpu.CompilerParams(
            collective_id=0, has_side_effects=True, vmem_limit_bytes=60 * 1024 * 1024
        ),
    )(
        ids,
        total,
        tokens,
        norm_gain_vector.reshape(1, width),
        gate_weight,
        up_weight,
        down_weight,
        pack,
        low,
        high,
    )


def solution(mesh):
    in_specs = (
        P("req", "mlp"),
        P(),
        P(None, "mlp"),
        P(None, "mlp"),
        P("mlp", None),
        P("req", None, None),
        P("req", None, None, "mlp"),
        P("req", "mlp", None),
        P("req", None, None),
        P(),
        P(),
        P(),
    )
    return jax.shard_map(
        on_device, mesh=mesh, in_specs=in_specs, out_specs=P("req", "mlp"), check_vma=False
    )
```

```python
import functools

import jax
import jax.numpy as jnp
from jax import lax
from jax.experimental import pallas as pl
from jax.experimental.pallas import tpu as pltpu
from jax.sharding import PartitionSpec as P

EPSILON = 1e-06
CHUNKS = 4
MESH = pl.DeviceIdType.MESH
NT = (((1,), (1,)), ((), ()))


def kernel(
    groups,
    owned,
    rank,
    slots,
    lengths_ref,
    slot_ref,
    chosen_ref,
    tokens_ref,
    gain_ref,
    gate_ref,
    up_ref,
    down_ref,
    a_ref,
    b_ref,
    da_ref,
    db_ref,
    out_ref,
    gate_v,
    up_v,
    down_v,
    whole,
    normed,
    hidden,
    maps,
    maps_sib,
    a_sel,
    bg_sel,
    bu_sel,
    da_sel,
    db_sel,
    own_part,
    sib_out,
    sib_in,
    far_out,
    far_in,
    up_s,
    dn_s,
    line_r,
    cross_s,
    cross_r,
    af_s,
    af_r,
    ts_s,
    ts_r,
    tc_s,
    tc_r,
    tf_s,
    tf_r,
    rs_s,
    rs_r,
    rc_s,
    rc_r,
    local_sem,
):
    r = lax.axis_index("req")
    m = lax.axis_index("mlp")
    half = lax.rem(m, 2)
    sib = m + 1 - 2 * half
    side = m // 2
    far = m + 2 - 4 * side
    diag = sib + 2 - 4 * side
    lane = lax.rem(r, 2)
    partner = r + 1 - 2 * lane
    place = r // 2
    places = groups // 2
    rows, cols = tokens_ref.shape
    rc = rows // CHUNKS
    hwidth = maps_sib.shape[2]
    inner = gate_v.shape[1]
    span = slots * rank

    def local(i, src, dst):
        return pltpu.make_async_copy(src, dst, local_sem.at[i])

    def remote(src, dst, ss, rs, axis, dev):
        return pltpu.make_async_remote_copy(
            src_ref=src,
            dst_ref=dst,
            send_sem=ss,
            recv_sem=rs,
            device_id={axis: dev},
            device_id_type=MESH,
        )

    def rows_of(k):
        return pl.ds(pl.multiple_of(k * rc, rc), rc)

    def up_copy(i):
        slot = maps.at[2 * i + lane]
        return remote(slot, slot, up_s.at[i], line_r.at[i], "req", r + 2)

    def down_copy(i):
        slot = maps.at[2 * i + lane]
        return remote(slot, slot, dn_s.at[i], line_r.at[i], "req", r - 2)

    def cross_copy(i, side_of):
        slot = maps.at[2 * i + side_of]
        return remote(slot, slot, cross_s.at[i], cross_r.at[i], "req", partner)

    def af_copy(g):
        return remote(
            maps.at[g, :, pl.ds(0, hwidth)], maps_sib.at[g], af_s.at[g], af_r.at[g], "mlp", sib
        )

    def tok_sib(k, who):
        return remote(
            tokens_ref.at[rows_of(k)], whole.at[who, rows_of(k)], ts_s.at[k], ts_r.at[k], "mlp", sib
        )

    def tok_far(k, who):
        return remote(
            tokens_ref.at[rows_of(k)], whole.at[who, rows_of(k)], tc_s.at[k], tc_r.at[k], "mlp", far
        )

    def tok_fwd(k, who):
        return remote(
            whole.at[far, rows_of(k)], whole.at[who, rows_of(k)], tf_s.at[k], tf_r.at[k], "mlp", sib
        )

    def part_sib(k):
        return remote(sib_out.at[k], sib_in.at[k], rs_s.at[k], rs_r.at[k], "mlp", sib)

    def part_far(k):
        return remote(far_out.at[k], far_in.at[k], rc_s.at[k], rc_r.at[k], "mlp", far)

    w_copies = [
        local(0, gate_ref, gate_v),
        local(1, up_ref, up_v),
        local(2, down_ref, down_v),
        local(3, tokens_ref, whole.at[m]),
    ]
    mine = pl.ds(pl.multiple_of(half * hwidth, hwidth), hwidth)
    other = pl.ds(pl.multiple_of((1 - half) * hwidth, hwidth), hwidth)
    per = 3 * rank
    packs = []
    for o in range(owned):
        first, last = pl.ds(o * per, 2 * rank), pl.ds(o * per + 2 * rank, rank)
        left, right = pl.ds(0, hwidth), pl.ds(hwidth, inner)
        packs += [
            (a_ref.at[o, :, mine], maps.at[r, first, left]),
            (b_ref.at[o], maps.at[r, first, right]),
            (da_ref.at[o], maps.at[r, last, right]),
            (db_ref.at[o, :, mine], maps.at[r, last, left]),
        ]
    packs = [local(4 + i, src, dst) for i, (src, dst) in enumerate(packs)]
    for copy in packs:
        copy.start()

    barrier = pltpu.get_barrier_semaphore()

    def greet(axis, dev):
        pl.semaphore_signal(barrier, inc=1, device_id={axis: dev}, device_id_type=MESH)

    greet("mlp", sib)
    greet("mlp", far)
    greet("req", partner)
    inner_up = place < places - 1
    inner_down = place > 0

    @pl.when(inner_up)
    def _():
        greet("req", r + 2)

    @pl.when(inner_down)
    def _():
        greet("req", r - 2)

    below = (place + places - 1) // places
    above = (2 * (places - 1) - place) // places
    pl.semaphore_wait(barrier, 3 + below + above)

    def each(n, start=0):
        def deco(f):
            def body(i, carry):
                f(i)
                return carry

            lax.fori_loop(start, n, body, 0)

        return deco

    @each(CHUNKS)
    def _(k):
        tok_far(k, m).start()
        tok_sib(k, m).start()

    def pass_on(k):
        tok_far(k, far).wait_recv()
        tok_fwd(k, far).start()

    for copy in packs:
        copy.wait()

    @pl.when(inner_up)
    def _():
        up_copy(place).start()

    @pl.when(inner_down)
    def _():
        down_copy(place).start()

    cross_copy(place, lane).start()
    af_copy(r).start()

    for j in (3, 0, 1, 2):
        w_copies[j].start()
    pass_on(0)

    @each(places, 1)
    def _(d):
        @pl.when(place - d >= 0)
        def _():
            i = place - d
            up_copy(i).wait_recv()

            @pl.when(inner_up)
            def _():
                up_copy(i).start()

            cross_copy(i, lane).start()
            af_copy(2 * i + lane).start()

        @pl.when(place + d < places)
        def _():
            i = place + d
            down_copy(i).wait_recv()

            @pl.when(inner_down)
            def _():
                down_copy(i).start()

            cross_copy(i, lane).start()
            af_copy(2 * i + lane).start()

    @each(places)
    def _(i):
        cross_copy(i, 1 - lane).wait_recv()
        af_copy(2 * i + 1 - lane).start()

    @each(groups)
    def _(g):
        af_copy(g).wait_recv()

    bg_sel[...] = jnp.zeros_like(bg_sel)
    bu_sel[...] = jnp.zeros_like(bu_sel)
    column = lax.broadcasted_iota(jnp.int32, (1, 2 * span), 1)
    column = jnp.where(column < span, column, column - span)
    low = jnp.zeros((1, 2 * span), jnp.int32)
    high = jnp.zeros((1, 2 * span), jnp.int32)
    total = 0
    for q in range(slots):
        own_q = (column >= q * rank) & (column < (q + 1) * rank)
        low = jnp.where(own_q, total, low)
        total = total + lengths_ref[q, r]
        high = jnp.where(own_q, total, high)
        chosen = chosen_ref[slot_ref[q, r]]
        g = chosen // owned if owned > 1 else chosen
        at = pl.ds(q * rank, rank)
        at2 = pl.ds(span + q * rank, rank)
        row0 = lax.rem(chosen, owned) * per if owned > 1 else 0
        for dst, part in ((mine, maps), (other, maps_sib)):
            a_sel[at, dst] = part[g, pl.ds(row0, rank), 0:hwidth]
            a_sel[at2, dst] = part[g, pl.ds(row0 + rank, rank), 0:hwidth]
            db = part[g, pl.ds(row0 + 2 * rank, rank), 0:hwidth]
            db_sel[at, dst] = db
            db_sel[at2, dst] = db
        bg_sel[at, :] = maps[g, pl.ds(row0, rank), hwidth : hwidth + inner]
        bu_sel[at2, :] = maps[g, pl.ds(row0 + rank, rank), hwidth : hwidth + inner]
        da = maps[g, pl.ds(row0 + 2 * rank, rank), hwidth : hwidth + inner]
        da_sel[at, :] = da
        da_sel[at2, :] = da
    for j in range(4):
        w_copies[j].wait()

    parts = whole.shape[0]
    f32 = jnp.float32
    gain_row = gain_ref[...].astype(f32).reshape(1, -1)

    def reduce_far(k):
        part_sib(k).wait_recv()
        far_out[k] = (own_part[k, 0] + sib_in[k, 0].astype(f32)).astype(jnp.bfloat16)
        part_far(k).start()

    @each(CHUNKS)
    def _(k):
        here = rows_of(k)

        @pl.when(k < CHUNKS - 1)
        def _():
            pass_on(k + 1)

        tok_sib(k, sib).wait_recv()
        tok_fwd(k, diag).wait_recv()
        squares = jnp.zeros((rc, 1), f32)
        for b in range(parts):
            x = whole[b, here, :].astype(f32)
            squares += jnp.sum(x * x, axis=1, keepdims=True)
        scale = lax.rsqrt(squares / (parts * cols) + EPSILON)
        for b in range(parts):
            x = whole[b, here, :].astype(f32)
            gain = gain_row[:, b * cols : (b + 1) * cols]
            normed[:, b * cols : (b + 1) * cols] = (x * scale * gain).astype(jnp.bfloat16)
        at = lax.broadcasted_iota(jnp.int32, (rc, 2 * span), 0) + k * rc
        live = (at >= low) & (at < high)
        low_rank = lax.dot_general(normed[...], a_sel[...], NT, preferred_element_type=f32)
        low_rank = jnp.where(live, low_rank, 0.0).astype(jnp.bfloat16)
        for n0 in range(0, inner, 256):
            n1 = min(n0 + 256, inner)
            g = jnp.dot(normed[...], gate_v[:, n0:n1], preferred_element_type=f32)
            g += jnp.dot(low_rank, bg_sel[:, n0:n1], preferred_element_type=f32)
            u = jnp.dot(normed[...], up_v[:, n0:n1], preferred_element_type=f32)
            u += jnp.dot(low_rank, bu_sel[:, n0:n1], preferred_element_type=f32)
            hidden[:, n0:n1] = (jax.nn.silu(g) * u).astype(jnp.bfloat16)
        down_rank = lax.dot_general(hidden[...], da_sel[...], NT, preferred_element_type=f32)
        down_rank = jnp.where(live, down_rank, 0.0)
        coarse = down_rank.astype(jnp.bfloat16).astype(f32)
        lane = lax.broadcasted_iota(jnp.int32, (rc, 2 * span), 1)
        down_rank = jnp.where(lane < span, coarse, down_rank - coarse).astype(jnp.bfloat16)

        def part_of(b):
            there = pl.ds(pl.multiple_of(b * cols, cols), cols)
            return jnp.dot(hidden[...], down_v[:, there], preferred_element_type=f32) + jnp.dot(
                down_rank, db_sel[:, there], preferred_element_type=f32
            )

        sib_out[k, 0] = part_of(diag).astype(jnp.bfloat16)
        sib_out[k, 1] = part_of(sib).astype(jnp.bfloat16)
        part_sib(k).start()
        own_part[k, 0] = part_of(far)

        @pl.when(k > 0)
        def _():
            reduce_far(k - 1)

        own_part[k, 1] = part_of(m)

    reduce_far(CHUNKS - 1)

    @each(CHUNKS)
    def _(k):
        here = rows_of(k)
        part_far(k).wait_recv()
        branch = own_part[k, 1] + sib_in[k, 1].astype(f32) + far_in[k].astype(f32)
        branch = branch.astype(jnp.bfloat16).astype(f32)
        at = lax.broadcasted_iota(jnp.int32, (rc, cols), 0) + k * rc
        x = whole[m, here, :].astype(f32)
        out_ref[here, :] = jnp.where(at < total, x + branch, x).astype(out_ref.dtype)

    @each(CHUNKS)
    def _(k):
        tok_far(k, m).wait_send()
        tok_sib(k, m).wait_send()
        tok_fwd(k, far).wait_send()
        part_sib(k).wait_send()
        part_far(k).wait_send()

    @each(places)
    def _(i):
        cross_copy(i, lane).wait_send()

        @pl.when(inner_up & (i <= place))
        def _():
            up_copy(i).wait_send()

        @pl.when(inner_down & (i >= place))
        def _():
            down_copy(i).wait_send()

    @each(groups)
    def _(g):
        af_copy(g).wait_send()


def on_device(
    tokens,
    norm_gain_vector,
    gate_weight,
    up_weight,
    down_weight,
    gate_up_input_maps,
    gate_up_output_maps,
    down_input_maps,
    down_output_maps,
    lengths,
    request_adapter_slot,
    selected,
):
    groups = lax.axis_size("req")
    parts = lax.axis_size("mlp")
    rows, cols = tokens.shape
    owned, rank, width = down_output_maps.shape
    inner = gate_weight.shape[1]
    slots = lengths.shape[1]
    span = slots * rank
    hwidth = width // 2
    packed = (owned * 3 * rank, hwidth + inner)
    bf16 = jnp.bfloat16

    rc = rows // CHUNKS
    vm, sm, hbm = (
        pl.BlockSpec(memory_space=s) for s in (pltpu.VMEM, pltpu.SMEM, pl.ANY)
    )
    dma = pltpu.SemaphoreType.DMA
    return pl.pallas_call(
        functools.partial(kernel, groups, owned, rank, slots),
        out_shape=jax.ShapeDtypeStruct((rows, cols), tokens.dtype),
        in_specs=[sm, sm, sm, hbm, vm] + [hbm] * 7,
        out_specs=vm,
        scratch_shapes=[
            pltpu.VMEM((width, inner), bf16),
            pltpu.VMEM((width, inner), bf16),
            pltpu.VMEM((inner, width), bf16),
            pltpu.VMEM((parts, rows, cols), bf16),
            pltpu.VMEM((rc, width), bf16),
            pltpu.VMEM((rc, inner), bf16),
            pltpu.VMEM((groups,) + packed, bf16),
            pltpu.VMEM((groups, packed[0], hwidth), bf16),
            pltpu.VMEM((2 * span, width), bf16),
            pltpu.VMEM((2 * span, inner), bf16),
            pltpu.VMEM((2 * span, inner), bf16),
            pltpu.VMEM((2 * span, inner), bf16),
            pltpu.VMEM((2 * span, width), bf16),
            pltpu.VMEM((CHUNKS, 2, rc, cols), jnp.float32),
            pltpu.VMEM((CHUNKS, 2, rc, cols), bf16),
            pltpu.VMEM((CHUNKS, 2, rc, cols), bf16),
            pltpu.VMEM((CHUNKS, rc, cols), bf16),
            pltpu.VMEM((CHUNKS, rc, cols), bf16),
            dma((groups // 2,)),
            dma((groups // 2,)),
            dma((groups // 2,)),
            dma((groups // 2,)),
            dma((groups // 2,)),
            dma((groups,)),
            dma((groups,)),
        ]
        + [dma((CHUNKS,)) for _ in range(10)]
        + [dma((4 + 4 * owned,))],
        compiler_params=pltpu.CompilerParams(
            collective_id=0, has_side_effects=True, vmem_limit_bytes=60 * 1024 * 1024
        ),
    )(
        lengths.T,
        request_adapter_slot.T,
        selected,
        tokens,
        norm_gain_vector,
        gate_weight,
        up_weight,
        down_weight,
        jnp.swapaxes(gate_up_input_maps, 1, 2),
        gate_up_output_maps.reshape(owned, 2 * rank, inner),
        jnp.swapaxes(down_input_maps, 1, 2),
        down_output_maps,
    )


def solution(mesh):
    in_specs = (
        P("req", "mlp"),
        P(),
        P(None, "mlp"),
        P(None, "mlp"),
        P("mlp", None),
        P("req", None, None),
        P("req", None, None, "mlp"),
        P("req", "mlp", None),
        P("req", None, None),
        P(),
        P(),
        P(),
    )
    return jax.shard_map(
        on_device, mesh=mesh, in_specs=in_specs, out_specs=P("req", "mlp"), check_vma=False
    )
```

```python
import functools

import jax
import jax.numpy as jnp
from jax import lax
from jax.experimental import pallas as pl
from jax.experimental.pallas import tpu as pltpu
from jax.sharding import PartitionSpec as P

EPSILON = 1e-06
CHUNKS = 4
MESH = pl.DeviceIdType.MESH
NT = (((1,), (1,)), ((), ()))


def kernel(
    groups,
    owned,
    rank,
    slots,
    lengths_ref,
    slot_ref,
    chosen_ref,
    tokens_ref,
    gain_ref,
    gate_ref,
    up_ref,
    down_ref,
    a_ref,
    b_ref,
    da_ref,
    db_ref,
    out_ref,
    gate_v,
    up_v,
    down_v,
    whole,
    normed,
    gate_sum,
    up_sum,
    hidden,
    maps,
    maps_sib,
    a_sel,
    bg_sel,
    bu_sel,
    da_sel,
    db_sel,
    own_part,
    sib_out,
    sib_in,
    far_out,
    far_in,
    up_s,
    dn_s,
    line_r,
    cross_s,
    cross_r,
    af_s,
    af_r,
    ts_s,
    ts_r,
    tc_s,
    tc_r,
    tf_s,
    tf_r,
    rs_s,
    rs_r,
    rc_s,
    rc_r,
    local_sem,
):
    r = lax.axis_index("req")
    m = lax.axis_index("mlp")
    half = lax.rem(m, 2)
    sib = m + 1 - 2 * half
    side = m // 2
    far = m + 2 - 4 * side
    diag = sib + 2 - 4 * side
    lane = lax.rem(r, 2)
    partner = r + 1 - 2 * lane
    place = r // 2
    places = groups // 2
    rows, cols = tokens_ref.shape
    rc = rows // CHUNKS
    hwidth = maps_sib.shape[2]
    inner = gate_v.shape[1]
    span = slots * rank

    def local(i, src, dst):
        return pltpu.make_async_copy(src, dst, local_sem.at[i])

    def remote(src, dst, ss, rs, axis, dev):
        return pltpu.make_async_remote_copy(
            src_ref=src,
            dst_ref=dst,
            send_sem=ss,
            recv_sem=rs,
            device_id={axis: dev},
            device_id_type=MESH,
        )

    def rows_of(k):
        return pl.ds(pl.multiple_of(k * rc, rc), rc)

    def up_copy(i):
        slot = maps.at[2 * i + lane]
        return remote(slot, slot, up_s.at[i], line_r.at[i], "req", r + 2)

    def down_copy(i):
        slot = maps.at[2 * i + lane]
        return remote(slot, slot, dn_s.at[i], line_r.at[i], "req", r - 2)

    def cross_copy(i, side_of):
        slot = maps.at[2 * i + side_of]
        return remote(slot, slot, cross_s.at[i], cross_r.at[i], "req", partner)

    def af_copy(g):
        return remote(
            maps.at[g, :, pl.ds(0, hwidth)], maps_sib.at[g], af_s.at[g], af_r.at[g], "mlp", sib
        )

    def tok_sib(k, who):
        return remote(
            tokens_ref.at[rows_of(k)], whole.at[who, rows_of(k)], ts_s.at[k], ts_r.at[k], "mlp", sib
        )

    def tok_far(k, who):
        return remote(
            tokens_ref.at[rows_of(k)], whole.at[who, rows_of(k)], tc_s.at[k], tc_r.at[k], "mlp", far
        )

    def tok_fwd(k, who):
        return remote(
            whole.at[far, rows_of(k)], whole.at[who, rows_of(k)], tf_s.at[k], tf_r.at[k], "mlp", sib
        )

    def part_sib(k):
        return remote(sib_out.at[k], sib_in.at[k], rs_s.at[k], rs_r.at[k], "mlp", sib)

    def part_far(k):
        return remote(far_out.at[k], far_in.at[k], rc_s.at[k], rc_r.at[k], "mlp", far)

    w_copies = [
        local(0, gate_ref, gate_v),
        local(1, up_ref, up_v),
        local(2, down_ref, down_v),
        local(3, tokens_ref, whole.at[m]),
    ]
    mine = pl.ds(pl.multiple_of(half * hwidth, hwidth), hwidth)
    other = pl.ds(pl.multiple_of((1 - half) * hwidth, hwidth), hwidth)
    per = 3 * rank
    packs = []
    for o in range(owned):
        first, last = pl.ds(o * per, 2 * rank), pl.ds(o * per + 2 * rank, rank)
        left, right = pl.ds(0, hwidth), pl.ds(hwidth, inner)
        packs += [
            (a_ref.at[o, :, mine], maps.at[r, first, left]),
            (b_ref.at[o], maps.at[r, first, right]),
            (da_ref.at[o], maps.at[r, last, right]),
            (db_ref.at[o, :, mine], maps.at[r, last, left]),
        ]
    packs = [local(4 + i, src, dst) for i, (src, dst) in enumerate(packs)]
    for copy in packs:
        copy.start()

    barrier = pltpu.get_barrier_semaphore()

    def greet(axis, dev):
        pl.semaphore_signal(barrier, inc=1, device_id={axis: dev}, device_id_type=MESH)

    greet("mlp", sib)
    greet("mlp", far)
    greet("req", partner)
    inner_up = place < places - 1
    inner_down = place > 0

    @pl.when(inner_up)
    def _():
        greet("req", r + 2)

    @pl.when(inner_down)
    def _():
        greet("req", r - 2)

    below = (place + places - 1) // places
    above = (2 * (places - 1) - place) // places
    pl.semaphore_wait(barrier, 3 + below + above)

    def each(n, start=0):
        def deco(f):
            def body(i, carry):
                f(i)
                return carry

            lax.fori_loop(start, n, body, 0)

        return deco

    @each(CHUNKS)
    def _(k):
        tok_far(k, m).start()
        tok_sib(k, m).start()

    def pass_on(k):
        tok_far(k, far).wait_recv()
        tok_fwd(k, far).start()

    for copy in packs:
        copy.wait()

    @pl.when(inner_up)
    def _():
        up_copy(place).start()

    @pl.when(inner_down)
    def _():
        down_copy(place).start()

    cross_copy(place, lane).start()
    af_copy(r).start()

    for j in (3, 0, 1, 2):
        w_copies[j].start()
    parts = whole.shape[0]
    f32 = jnp.float32
    gain_row = gain_ref[...].astype(f32).reshape(1, -1)
    early = CHUNKS - 1

    def relay(d, carry):
        @pl.when(place - d >= 0)
        def _():
            i = place - d
            up_copy(i).wait_recv()

            @pl.when(inner_up)
            def _():
                up_copy(i).start()

            cross_copy(i, lane).start()
            af_copy(2 * i + lane).start()

        @pl.when(place + d < places)
        def _():
            i = place + d
            down_copy(i).wait_recv()

            @pl.when(inner_down)
            def _():
                down_copy(i).start()

            cross_copy(i, lane).start()
            af_copy(2 * i + lane).start()

        return carry

    def base(k):
        here = rows_of(k)
        tok_sib(k, sib).wait_recv()
        tok_fwd(k, diag).wait_recv()
        squares = jnp.zeros((rc, 1), f32)
        for b in range(parts):
            x = whole[b, here, :].astype(f32)
            squares += jnp.sum(x * x, axis=1, keepdims=True)
        scale = lax.rsqrt(squares / (parts * cols) + EPSILON)
        for b in range(parts):
            x = whole[b, here, :].astype(f32)
            gain = gain_row[:, b * cols : (b + 1) * cols]
            normed[k, :, b * cols : (b + 1) * cols] = (x * scale * gain).astype(jnp.bfloat16)
        for n0 in range(0, inner, 256):
            n1 = min(n0 + 256, inner)
            gate_sum[k, :, n0:n1] = jnp.dot(
                normed[k], gate_v[:, n0:n1], preferred_element_type=f32
            )
            up_sum[k, :, n0:n1] = jnp.dot(normed[k], up_v[:, n0:n1], preferred_element_type=f32)

    for copy in w_copies:
        copy.wait()
    pass_on(0)

    @each(early)
    def _(j):
        first = 1 + (places - 1) * j // early
        last = 1 + (places - 1) * (j + 1) // early
        lax.fori_loop(first, last, relay, 0)
        base(j)

        @pl.when(j < early - 1)
        def _():
            pass_on(j + 1)

    @each(places)
    def _(i):
        cross_copy(i, 1 - lane).wait_recv()
        af_copy(2 * i + 1 - lane).start()

    @each(groups)
    def _(g):
        af_copy(g).wait_recv()

    bg_sel[...] = jnp.zeros_like(bg_sel)
    bu_sel[...] = jnp.zeros_like(bu_sel)
    column = lax.broadcasted_iota(jnp.int32, (1, 2 * span), 1)
    column = jnp.where(column < span, column, column - span)
    low = jnp.zeros((1, 2 * span), jnp.int32)
    high = jnp.zeros((1, 2 * span), jnp.int32)
    total = 0
    for q in range(slots):
        own_q = (column >= q * rank) & (column < (q + 1) * rank)
        low = jnp.where(own_q, total, low)
        total = total + lengths_ref[q, r]
        high = jnp.where(own_q, total, high)
        chosen = chosen_ref[slot_ref[q, r]]
        g = chosen // owned if owned > 1 else chosen
        at = pl.ds(q * rank, rank)
        at2 = pl.ds(span + q * rank, rank)
        row0 = lax.rem(chosen, owned) * per if owned > 1 else 0
        for dst, part in ((mine, maps), (other, maps_sib)):
            a_sel[at, dst] = part[g, pl.ds(row0, rank), 0:hwidth]
            a_sel[at2, dst] = part[g, pl.ds(row0 + rank, rank), 0:hwidth]
            db = part[g, pl.ds(row0 + 2 * rank, rank), 0:hwidth]
            db_sel[at, dst] = db
            db_sel[at2, dst] = db
        bg_sel[at, :] = maps[g, pl.ds(row0, rank), hwidth : hwidth + inner]
        bu_sel[at2, :] = maps[g, pl.ds(row0 + rank, rank), hwidth : hwidth + inner]
        da = maps[g, pl.ds(row0 + 2 * rank, rank), hwidth : hwidth + inner]
        da_sel[at, :] = da
        da_sel[at2, :] = da
    def reduce_far(k):
        part_sib(k).wait_recv()
        far_out[k] = (own_part[k, 0] + sib_in[k, 0].astype(f32)).astype(jnp.bfloat16)
        part_far(k).start()

    @each(CHUNKS)
    def _(k):
        @pl.when(k == 1)
        def _():
            base(early)

        at = lax.broadcasted_iota(jnp.int32, (rc, 2 * span), 0) + k * rc
        live = (at >= low) & (at < high)
        low_rank = lax.dot_general(normed[k], a_sel[...], NT, preferred_element_type=f32)
        low_rank = jnp.where(live, low_rank, 0.0).astype(jnp.bfloat16)
        for n0 in range(0, inner, 256):
            n1 = min(n0 + 256, inner)
            g = gate_sum[k, :, n0:n1]
            g += jnp.dot(low_rank, bg_sel[:, n0:n1], preferred_element_type=f32)
            u = up_sum[k, :, n0:n1]
            u += jnp.dot(low_rank, bu_sel[:, n0:n1], preferred_element_type=f32)
            hidden[:, n0:n1] = (jax.nn.silu(g) * u).astype(jnp.bfloat16)
        down_rank = lax.dot_general(hidden[...], da_sel[...], NT, preferred_element_type=f32)
        down_rank = jnp.where(live, down_rank, 0.0)
        coarse = down_rank.astype(jnp.bfloat16).astype(f32)
        lane = lax.broadcasted_iota(jnp.int32, (rc, 2 * span), 1)
        down_rank = jnp.where(lane < span, coarse, down_rank - coarse).astype(jnp.bfloat16)

        def part_of(b):
            there = pl.ds(pl.multiple_of(b * cols, cols), cols)
            return jnp.dot(hidden[...], down_v[:, there], preferred_element_type=f32) + jnp.dot(
                down_rank, db_sel[:, there], preferred_element_type=f32
            )

        sib_out[k, 0] = part_of(diag).astype(jnp.bfloat16)
        sib_out[k, 1] = part_of(sib).astype(jnp.bfloat16)
        part_sib(k).start()

        @pl.when(k == 0)
        def _():
            pass_on(early)

        own_part[k, 0] = part_of(far)
        own_part[k, 1] = part_of(m)
        reduce_far(k)

    @each(CHUNKS)
    def _(k):
        here = rows_of(k)
        part_far(k).wait_recv()
        branch = own_part[k, 1] + sib_in[k, 1].astype(f32) + far_in[k].astype(f32)
        branch = branch.astype(jnp.bfloat16).astype(f32)
        at = lax.broadcasted_iota(jnp.int32, (rc, cols), 0) + k * rc
        x = whole[m, here, :].astype(f32)
        out_ref[here, :] = jnp.where(at < total, x + branch, x).astype(out_ref.dtype)

    @each(CHUNKS)
    def _(k):
        tok_far(k, m).wait_send()
        tok_sib(k, m).wait_send()
        tok_fwd(k, far).wait_send()
        part_sib(k).wait_send()
        part_far(k).wait_send()

    @each(places)
    def _(i):
        cross_copy(i, lane).wait_send()

        @pl.when(inner_up & (i <= place))
        def _():
            up_copy(i).wait_send()

        @pl.when(inner_down & (i >= place))
        def _():
            down_copy(i).wait_send()

    @each(groups)
    def _(g):
        af_copy(g).wait_send()


def on_device(
    tokens,
    norm_gain_vector,
    gate_weight,
    up_weight,
    down_weight,
    gate_up_input_maps,
    gate_up_output_maps,
    down_input_maps,
    down_output_maps,
    lengths,
    request_adapter_slot,
    selected,
):
    groups = lax.axis_size("req")
    parts = lax.axis_size("mlp")
    rows, cols = tokens.shape
    owned, rank, width = down_output_maps.shape
    inner = gate_weight.shape[1]
    slots = lengths.shape[1]
    span = slots * rank
    hwidth = width // 2
    packed = (owned * 3 * rank, hwidth + inner)
    bf16 = jnp.bfloat16

    rc = rows // CHUNKS
    vm, sm, hbm = (
        pl.BlockSpec(memory_space=s) for s in (pltpu.VMEM, pltpu.SMEM, pl.ANY)
    )
    dma = pltpu.SemaphoreType.DMA
    return pl.pallas_call(
        functools.partial(kernel, groups, owned, rank, slots),
        out_shape=jax.ShapeDtypeStruct((rows, cols), tokens.dtype),
        in_specs=[sm, sm, sm, hbm, vm] + [hbm] * 7,
        out_specs=vm,
        scratch_shapes=[
            pltpu.VMEM((width, inner), bf16),
            pltpu.VMEM((width, inner), bf16),
            pltpu.VMEM((inner, width), bf16),
            pltpu.VMEM((parts, rows, cols), bf16),
            pltpu.VMEM((CHUNKS, rc, width), bf16),
            pltpu.VMEM((CHUNKS, rc, inner), jnp.float32),
            pltpu.VMEM((CHUNKS, rc, inner), jnp.float32),
            pltpu.VMEM((rc, inner), bf16),
            pltpu.VMEM((groups,) + packed, bf16),
            pltpu.VMEM((groups, packed[0], hwidth), bf16),
            pltpu.VMEM((2 * span, width), bf16),
            pltpu.VMEM((2 * span, inner), bf16),
            pltpu.VMEM((2 * span, inner), bf16),
            pltpu.VMEM((2 * span, inner), bf16),
            pltpu.VMEM((2 * span, width), bf16),
            pltpu.VMEM((CHUNKS, 2, rc, cols), jnp.float32),
            pltpu.VMEM((CHUNKS, 2, rc, cols), bf16),
            pltpu.VMEM((CHUNKS, 2, rc, cols), bf16),
            pltpu.VMEM((CHUNKS, rc, cols), bf16),
            pltpu.VMEM((CHUNKS, rc, cols), bf16),
            dma((groups // 2,)),
            dma((groups // 2,)),
            dma((groups // 2,)),
            dma((groups // 2,)),
            dma((groups // 2,)),
            dma((groups,)),
            dma((groups,)),
        ]
        + [dma((CHUNKS,)) for _ in range(10)]
        + [dma((4 + 4 * owned,))],
        compiler_params=pltpu.CompilerParams(
            collective_id=0, has_side_effects=True, vmem_limit_bytes=60 * 1024 * 1024
        ),
    )(
        lengths.T,
        request_adapter_slot.T,
        selected,
        tokens,
        norm_gain_vector,
        gate_weight,
        up_weight,
        down_weight,
        jnp.swapaxes(gate_up_input_maps, 1, 2),
        gate_up_output_maps.reshape(owned, 2 * rank, inner),
        jnp.swapaxes(down_input_maps, 1, 2),
        down_output_maps,
    )


def solution(mesh):
    in_specs = (
        P("req", "mlp"),
        P(),
        P(None, "mlp"),
        P(None, "mlp"),
        P("mlp", None),
        P("req", None, None),
        P("req", None, None, "mlp"),
        P("req", "mlp", None),
        P("req", None, None),
        P(),
        P(),
        P(),
    )
    return jax.shard_map(
        on_device, mesh=mesh, in_specs=in_specs, out_specs=P("req", "mlp"), check_vma=False
    )
```

```python
import functools

import jax
import jax.numpy as jnp
from jax import lax
from jax.experimental import pallas as pl
from jax.experimental.pallas import tpu as pltpu
from jax.sharding import PartitionSpec as P

EPSILON = 1e-06
CHUNKS = 4
MESH = pl.DeviceIdType.MESH
NT = (((1,), (1,)), ((), ()))


def kernel(
    groups,
    owned,
    rank,
    slots,
    lengths_ref,
    slot_ref,
    chosen_ref,
    tokens_ref,
    gain_ref,
    gate_ref,
    up_ref,
    down_ref,
    a_ref,
    b_ref,
    da_ref,
    db_ref,
    out_ref,
    gate_v,
    up_v,
    down_v,
    whole,
    normed,
    gate_sum,
    up_sum,
    hidden,
    maps,
    maps_sib,
    a_sel,
    bg_sel,
    bu_sel,
    da_sel,
    db_sel,
    own_part,
    sib_out,
    sib_in,
    far_out,
    far_in,
    up_s,
    dn_s,
    line_r,
    cross_s,
    cross_r,
    af_s,
    af_r,
    ts_s,
    ts_r,
    tc_s,
    tc_r,
    tf_s,
    tf_r,
    rs_s,
    rs_r,
    rc_s,
    rc_r,
    local_sem,
):
    r = lax.axis_index("req")
    m = lax.axis_index("mlp")
    half = lax.rem(m, 2)
    sib = m + 1 - 2 * half
    side = m // 2
    far = m + 2 - 4 * side
    diag = sib + 2 - 4 * side
    lane = lax.rem(r, 2)
    partner = r + 1 - 2 * lane
    place = r // 2
    places = groups // 2
    rows, cols = tokens_ref.shape
    rc = rows // CHUNKS
    hwidth = maps_sib.shape[2]
    inner = gate_v.shape[1]
    span = slots * rank

    def local(i, src, dst):
        return pltpu.make_async_copy(src, dst, local_sem.at[i])

    def remote(src, dst, ss, rs, axis, dev):
        return pltpu.make_async_remote_copy(
            src_ref=src,
            dst_ref=dst,
            send_sem=ss,
            recv_sem=rs,
            device_id={axis: dev},
            device_id_type=MESH,
        )

    def rows_of(k):
        return pl.ds(pl.multiple_of(k * rc, rc), rc)

    def up_copy(i):
        slot = maps.at[2 * i + lane]
        return remote(slot, slot, up_s.at[i], line_r.at[i], "req", r + 2)

    def down_copy(i):
        slot = maps.at[2 * i + lane]
        return remote(slot, slot, dn_s.at[i], line_r.at[i], "req", r - 2)

    def cross_copy(i, side_of):
        slot = maps.at[2 * i + side_of]
        return remote(slot, slot, cross_s.at[i], cross_r.at[i], "req", partner)

    def af_copy(g):
        return remote(
            maps.at[g, :, pl.ds(0, hwidth)], maps_sib.at[g], af_s.at[g], af_r.at[g], "mlp", sib
        )

    def tok_sib(k, who):
        return remote(
            tokens_ref.at[rows_of(k)], whole.at[who, rows_of(k)], ts_s.at[k], ts_r.at[k], "mlp", sib
        )

    def tok_far(k, who):
        return remote(
            tokens_ref.at[rows_of(k)], whole.at[who, rows_of(k)], tc_s.at[k], tc_r.at[k], "mlp", far
        )

    def tok_fwd(k, who):
        return remote(
            whole.at[far, rows_of(k)], whole.at[who, rows_of(k)], tf_s.at[k], tf_r.at[k], "mlp", sib
        )

    def part_sib(k):
        return remote(sib_out.at[k], sib_in.at[k], rs_s.at[k], rs_r.at[k], "mlp", sib)

    def part_far(k):
        return remote(far_out.at[k], far_in.at[k], rc_s.at[k], rc_r.at[k], "mlp", far)

    w_copies = [
        local(0, gate_ref, gate_v),
        local(1, up_ref, up_v),
        local(2, down_ref, down_v),
        local(3, tokens_ref, whole.at[m]),
    ]
    mine = pl.ds(pl.multiple_of(half * hwidth, hwidth), hwidth)
    other = pl.ds(pl.multiple_of((1 - half) * hwidth, hwidth), hwidth)
    per = 3 * rank
    packs = []
    for o in range(owned):
        first, last = pl.ds(o * per, 2 * rank), pl.ds(o * per + 2 * rank, rank)
        left, right = pl.ds(0, hwidth), pl.ds(hwidth, inner)
        packs += [
            (a_ref.at[o, :, mine], maps.at[r, first, left]),
            (b_ref.at[o], maps.at[r, first, right]),
            (da_ref.at[o], maps.at[r, last, right]),
            (db_ref.at[o, :, mine], maps.at[r, last, left]),
        ]
    packs = [local(4 + i, src, dst) for i, (src, dst) in enumerate(packs)]
    for copy in packs:
        copy.start()

    barrier = pltpu.get_barrier_semaphore()

    def greet(axis, dev):
        pl.semaphore_signal(barrier, inc=1, device_id={axis: dev}, device_id_type=MESH)

    greet("mlp", sib)
    greet("mlp", far)
    greet("req", partner)
    inner_up = place < places - 1
    inner_down = place > 0

    @pl.when(inner_up)
    def _():
        greet("req", r + 2)

    @pl.when(inner_down)
    def _():
        greet("req", r - 2)

    below = (place + places - 1) // places
    above = (2 * (places - 1) - place) // places
    pl.semaphore_wait(barrier, 3 + below + above)

    def each(n, start=0):
        def deco(f):
            def body(i, carry):
                f(i)
                return carry

            lax.fori_loop(start, n, body, 0)

        return deco

    @each(CHUNKS)
    def _(k):
        tok_far(k, m).start()
        tok_sib(k, m).start()

    def pass_on(k):
        tok_far(k, far).wait_recv()
        tok_fwd(k, far).start()

    for copy in packs:
        copy.wait()

    @pl.when(inner_up)
    def _():
        up_copy(place).start()

    @pl.when(inner_down)
    def _():
        down_copy(place).start()

    cross_copy(place, lane).start()
    af_copy(r).start()

    for j in (3, 0, 1, 2):
        w_copies[j].start()
    parts = whole.shape[0]
    f32 = jnp.float32
    gain_row = gain_ref[...].astype(f32).reshape(1, -1)
    early = CHUNKS - 1

    def relay(d, carry):
        @pl.when(place - d >= 0)
        def _():
            i = place - d
            up_copy(i).wait_recv()

            @pl.when(inner_up)
            def _():
                up_copy(i).start()

            cross_copy(i, lane).start()
            af_copy(2 * i + lane).start()

        @pl.when(place + d < places)
        def _():
            i = place + d
            down_copy(i).wait_recv()

            @pl.when(inner_down)
            def _():
                down_copy(i).start()

            cross_copy(i, lane).start()
            af_copy(2 * i + lane).start()

        return carry

    def base(k):
        here = rows_of(k)
        tok_sib(k, sib).wait_recv()
        tok_fwd(k, diag).wait_recv()
        squares = jnp.zeros((rc, 1), f32)
        for b in range(parts):
            x = whole[b, here, :].astype(f32)
            squares += jnp.sum(x * x, axis=1, keepdims=True)
        scale = lax.rsqrt(squares / (parts * cols) + EPSILON)
        for b in range(parts):
            x = whole[b, here, :].astype(f32)
            gain = gain_row[:, b * cols : (b + 1) * cols]
            normed[k, :, b * cols : (b + 1) * cols] = (x * scale * gain).astype(jnp.bfloat16)
        for n0 in range(0, inner, 256):
            n1 = min(n0 + 256, inner)
            gate_sum[k, :, n0:n1] = jnp.dot(
                normed[k], gate_v[:, n0:n1], preferred_element_type=f32
            )
            up_sum[k, :, n0:n1] = jnp.dot(normed[k], up_v[:, n0:n1], preferred_element_type=f32)

    for copy in w_copies:
        copy.wait()
    pass_on(0)

    @each(early)
    def _(j):
        first = 1 + (places - 1) * j // early
        last = 1 + (places - 1) * (j + 1) // early
        lax.fori_loop(first, last, relay, 0)
        base(j)

        @pl.when(j < early - 1)
        def _():
            pass_on(j + 1)

    @each(places)
    def _(i):
        cross_copy(i, 1 - lane).wait_recv()
        af_copy(2 * i + 1 - lane).start()

    @each(groups)
    def _(g):
        af_copy(g).wait_recv()

    bg_sel[...] = jnp.zeros_like(bg_sel)
    bu_sel[...] = jnp.zeros_like(bu_sel)
    column = lax.broadcasted_iota(jnp.int32, (1, 2 * span), 1)
    column = jnp.where(column < span, column, column - span)
    low = jnp.zeros((1, 2 * span), jnp.int32)
    high = jnp.zeros((1, 2 * span), jnp.int32)
    total = 0
    for q in range(slots):
        own_q = (column >= q * rank) & (column < (q + 1) * rank)
        low = jnp.where(own_q, total, low)
        total = total + lengths_ref[q, r]
        high = jnp.where(own_q, total, high)
        chosen = chosen_ref[slot_ref[q, r]]
        g = chosen // owned if owned > 1 else chosen
        at = pl.ds(q * rank, rank)
        at2 = pl.ds(span + q * rank, rank)
        row0 = lax.rem(chosen, owned) * per if owned > 1 else 0
        for dst, part in ((mine, maps), (other, maps_sib)):
            a_sel[at, dst] = part[g, pl.ds(row0, rank), 0:hwidth]
            a_sel[at2, dst] = part[g, pl.ds(row0 + rank, rank), 0:hwidth]
            db = part[g, pl.ds(row0 + 2 * rank, rank), 0:hwidth]
            db_sel[at, dst] = db
            db_sel[at2, dst] = db
        bg_sel[at, :] = maps[g, pl.ds(row0, rank), hwidth : hwidth + inner]
        bu_sel[at2, :] = maps[g, pl.ds(row0 + rank, rank), hwidth : hwidth + inner]
        da = maps[g, pl.ds(row0 + 2 * rank, rank), hwidth : hwidth + inner]
        da_sel[at, :] = da
        da_sel[at2, :] = da
    def reduce_far(k):
        part_sib(k).wait_recv()
        far_out[k] = (own_part[k, 0] + sib_in[k, 0].astype(f32)).astype(jnp.bfloat16)
        part_far(k).start()

    @each(CHUNKS)
    def _(k):
        @pl.when(k == early - 1)
        def _():
            base(early)

        at = lax.broadcasted_iota(jnp.int32, (rc, 2 * span), 0) + k * rc
        live = (at >= low) & (at < high)
        low_rank = lax.dot_general(normed[k], a_sel[...], NT, preferred_element_type=f32)
        low_rank = jnp.where(live, low_rank, 0.0).astype(jnp.bfloat16)
        for n0 in range(0, inner, 256):
            n1 = min(n0 + 256, inner)
            g = gate_sum[k, :, n0:n1]
            g += jnp.dot(low_rank, bg_sel[:, n0:n1], preferred_element_type=f32)
            u = up_sum[k, :, n0:n1]
            u += jnp.dot(low_rank, bu_sel[:, n0:n1], preferred_element_type=f32)
            hidden[:, n0:n1] = (jax.nn.silu(g) * u).astype(jnp.bfloat16)
        down_rank = lax.dot_general(hidden[...], da_sel[...], NT, preferred_element_type=f32)
        down_rank = jnp.where(live, down_rank, 0.0)
        coarse = down_rank.astype(jnp.bfloat16).astype(f32)
        lane = lax.broadcasted_iota(jnp.int32, (rc, 2 * span), 1)
        down_rank = jnp.where(lane < span, coarse, down_rank - coarse).astype(jnp.bfloat16)

        def part_of(b):
            there = pl.ds(pl.multiple_of(b * cols, cols), cols)
            return jnp.dot(hidden[...], down_v[:, there], preferred_element_type=f32) + jnp.dot(
                down_rank, db_sel[:, there], preferred_element_type=f32
            )

        sib_out[k, 0] = part_of(diag).astype(jnp.bfloat16)
        sib_out[k, 1] = part_of(sib).astype(jnp.bfloat16)
        part_sib(k).start()

        @pl.when(k == 0)
        def _():
            pass_on(early)

        own_part[k, 0] = part_of(far)
        own_part[k, 1] = part_of(m)
        reduce_far(k)

    @each(CHUNKS)
    def _(k):
        here = rows_of(k)
        part_far(k).wait_recv()
        branch = own_part[k, 1] + sib_in[k, 1].astype(f32) + far_in[k].astype(f32)
        branch = branch.astype(jnp.bfloat16).astype(f32)
        at = lax.broadcasted_iota(jnp.int32, (rc, cols), 0) + k * rc
        x = whole[m, here, :].astype(f32)
        out_ref[here, :] = jnp.where(at < total, x + branch, x).astype(out_ref.dtype)

    @each(CHUNKS)
    def _(k):
        tok_far(k, m).wait_send()
        tok_sib(k, m).wait_send()
        tok_fwd(k, far).wait_send()
        part_sib(k).wait_send()
        part_far(k).wait_send()

    @each(places)
    def _(i):
        cross_copy(i, lane).wait_send()

        @pl.when(inner_up & (i <= place))
        def _():
            up_copy(i).wait_send()

        @pl.when(inner_down & (i >= place))
        def _():
            down_copy(i).wait_send()

    @each(groups)
    def _(g):
        af_copy(g).wait_send()


def on_device(
    tokens,
    norm_gain_vector,
    gate_weight,
    up_weight,
    down_weight,
    gate_up_input_maps,
    gate_up_output_maps,
    down_input_maps,
    down_output_maps,
    lengths,
    request_adapter_slot,
    selected,
):
    groups = lax.axis_size("req")
    parts = lax.axis_size("mlp")
    rows, cols = tokens.shape
    owned, rank, width = down_output_maps.shape
    inner = gate_weight.shape[1]
    slots = lengths.shape[1]
    span = slots * rank
    hwidth = width // 2
    packed = (owned * 3 * rank, hwidth + inner)
    bf16 = jnp.bfloat16

    rc = rows // CHUNKS
    vm, sm, hbm = (
        pl.BlockSpec(memory_space=s) for s in (pltpu.VMEM, pltpu.SMEM, pl.ANY)
    )
    dma = pltpu.SemaphoreType.DMA
    return pl.pallas_call(
        functools.partial(kernel, groups, owned, rank, slots),
        out_shape=jax.ShapeDtypeStruct((rows, cols), tokens.dtype),
        in_specs=[sm, sm, sm, hbm, vm] + [hbm] * 7,
        out_specs=vm,
        scratch_shapes=[
            pltpu.VMEM((width, inner), bf16),
            pltpu.VMEM((width, inner), bf16),
            pltpu.VMEM((inner, width), bf16),
            pltpu.VMEM((parts, rows, cols), bf16),
            pltpu.VMEM((CHUNKS, rc, width), bf16),
            pltpu.VMEM((CHUNKS, rc, inner), jnp.float32),
            pltpu.VMEM((CHUNKS, rc, inner), jnp.float32),
            pltpu.VMEM((rc, inner), bf16),
            pltpu.VMEM((groups,) + packed, bf16),
            pltpu.VMEM((groups, packed[0], hwidth), bf16),
            pltpu.VMEM((2 * span, width), bf16),
            pltpu.VMEM((2 * span, inner), bf16),
            pltpu.VMEM((2 * span, inner), bf16),
            pltpu.VMEM((2 * span, inner), bf16),
            pltpu.VMEM((2 * span, width), bf16),
            pltpu.VMEM((CHUNKS, 2, rc, cols), jnp.float32),
            pltpu.VMEM((CHUNKS, 2, rc, cols), bf16),
            pltpu.VMEM((CHUNKS, 2, rc, cols), bf16),
            pltpu.VMEM((CHUNKS, rc, cols), bf16),
            pltpu.VMEM((CHUNKS, rc, cols), bf16),
            dma((groups // 2,)),
            dma((groups // 2,)),
            dma((groups // 2,)),
            dma((groups // 2,)),
            dma((groups // 2,)),
            dma((groups,)),
            dma((groups,)),
        ]
        + [dma((CHUNKS,)) for _ in range(10)]
        + [dma((4 + 4 * owned,))],
        compiler_params=pltpu.CompilerParams(
            collective_id=0, has_side_effects=True, vmem_limit_bytes=60 * 1024 * 1024
        ),
    )(
        lengths.T,
        request_adapter_slot.T,
        selected,
        tokens,
        norm_gain_vector,
        gate_weight,
        up_weight,
        down_weight,
        jnp.swapaxes(gate_up_input_maps, 1, 2),
        gate_up_output_maps.reshape(owned, 2 * rank, inner),
        jnp.swapaxes(down_input_maps, 1, 2),
        down_output_maps,
    )


def solution(mesh):
    in_specs = (
        P("req", "mlp"),
        P(),
        P(None, "mlp"),
        P(None, "mlp"),
        P("mlp", None),
        P("req", None, None),
        P("req", None, None, "mlp"),
        P("req", "mlp", None),
        P("req", None, None),
        P(),
        P(),
        P(),
    )
    return jax.shard_map(
        on_device, mesh=mesh, in_specs=in_specs, out_specs=P("req", "mlp"), check_vma=False
    )
```
